256 devices in a mesh: basis: 4 (over x_lo, core), tm: 64 (over y, x_hi, z).
Axes of the slice: x: 4 (x_hi: 2, x_lo: 2; x = x_hi * 2 + x_lo), y: 4, z: 8, core: 2. Of those that a mesh axis runs over, the one named last changes fastest.
Arguments:
- strain: bfloat16 [3, 32768], P(None, 'tm'), may hold values from -6 to 6
- basis_filters: bfloat16 [4096, 2048], P('basis'), may hold values from -0.125 to 0.125
- coefficients: bfloat16 [8192, 4096], P(('basis', 'tm')), may hold values from -0.375 to 0.375
Outputs:
- snr: bfloat16 [8192, 3, 8192], P('basis', None, 'tm')
The draws below stay inside these ranges and needn't reach their ends.
All inputs are finite; a program needn't handle non-finite values.
Results may differ from the reference program's by a relative error of at most 0.0049.
Values may be sent and summed in bfloat16 or wider, within the bound.
A program may use at most 128 MiB of HBM per device.

```python
import jax
import jax.numpy as jnp
from jax import lax

DET = 3
STRIDE = 4
FLEN = 2048
NBASIS = 4096
TEMPL = 8192
TIMES = 8192
SAMPLES = 32768
N_TM = 64


def with_spikes(entries, key, source, target, parts, factor):
    def block_of(axis_at):
        return (jnp.arange(entries.shape[axis_at]) // (entries.shape[axis_at] // parts)).reshape((-1,) + (1,) * (entries.ndim - 1 - axis_at))

    one_side = jax.random.permutation(key, parts)[block_of(target)]
    second = (block_of(target) + parts // 2) % parts
    return jnp.where((block_of(source) == one_side) | (block_of(source) == second), factor * entries, entries)


def block_scale(own_key, dims, split, low, largest):
    def one(axis_at, shards_of):
        heights = jax.random.uniform(jax.random.fold_in(jax.random.fold_in(own_key, 6), axis_at), (shards_of,), jnp.float32, low / len(split), largest / len(split))
        return jnp.repeat(jnp.exp(heights), dims[axis_at] // shards_of).reshape((-1,) + (1,) * (len(dims) - axis_at - 1))

    factor_of = one(*split[0])
    for cut in split[1:]:
        factor_of = factor_of * one(*cut)
    return factor_of


def scatter_about(key, extent, deviation, bound, pieces=(), dtype=jnp.bfloat16):
    values = deviation * jax.random.normal(key, extent, jnp.float32)
    if pieces:
        values = values * block_scale(key, extent, pieces, -0.22, 0.18)
    return jnp.clip(values, -bound, bound).astype(dtype)


def bell_draw_with(stream_key, extent, spread, limit, split, heavy, held_as=jnp.bfloat16):
    array = spread * jax.random.normal(stream_key, extent, jnp.float32)
    if split:
        array = array * block_scale(stream_key, extent, split, -0.22, 0.18)
    return jnp.clip(with_spikes(array, jax.random.fold_in(stream_key, 3), *heavy), -limit, limit).astype(held_as)


def setup_inputs(seed: int = 0) -> dict:
    seeds = jax.random.split(jax.random.key(seed), 4)
    return {
        "strain": scatter_about(seeds[0], (DET, SAMPLES), 1.0, 6.0, ((1, 64),)),
        "basis_filters": scatter_about(seeds[1], (NBASIS, FLEN), FLEN ** -0.5, 0.125, ((0, 4),)),
        "coefficients": bell_draw_with(seeds[2], (TEMPL, NBASIS), NBASIS ** -0.5, 0.375, ((0, 256),), (1, 0, 256, 6.0)),
    }


def reference(strain, basis_filters, coefficients):
    total_len = (TIMES + FLEN // STRIDE - 1) * STRIDE
    padded = jnp.pad(strain, ((0, 0), (0, total_len - SAMPLES)))
    window = padded.reshape(DET, total_len // STRIDE, STRIDE)
    phases = basis_filters.reshape(NBASIS, FLEN // STRIDE, STRIDE)
    correlation = lax.conv_general_dilated(window, phases, (1,), "VALID", dimension_numbers=("NHC", "OHI", "NCH"), preferred_element_type=jnp.float32).astype(jnp.bfloat16)
    flat_corr = jnp.transpose(correlation, (1, 0, 2)).reshape(NBASIS, DET * TIMES)
    row_blocks = coefficients.reshape(N_TM, TEMPL // N_TM, NBASIS)

    def one_block(rows_here):
        return jnp.dot(rows_here, flat_corr, preferred_element_type=jnp.float32).astype(jnp.bfloat16)

    result = lax.map(one_block, row_blocks)
    return result.reshape(TEMPL, DET, TIMES)
```

```python
import jax
import jax.numpy as jnp
from jax import lax
from jax.experimental import pallas as pl
from jax.experimental.pallas import tpu as pltpu
from jax.sharding import PartitionSpec as P

MESH = pl.DeviceIdType.MESH
STRIDE = 4
NZ, NY = 8, 4
LANES = 128
BF, F32 = jnp.bfloat16, jnp.float32


def kernel(
    s_ref, f_hbm, a_hbm, out_ref,
    a_all, s1, s_all, filt, hank, expand, corr, c1s, c1r, own, c2s, c2r, done,
    local_sem, s1_send, s1_recv, s2_send, s2_recv, row_send, row_recv,
    ring_send, ring_recv, c1_send, c1_recv, c2_send, c2_recv, c3_send, c3_recv, keep_sem,
):
    i = lax.axis_index("basis")
    j = lax.axis_index("tm")
    xl, core = i // 2, i % 2
    e, z = j // NZ, j % NZ
    y, xh = e // 2, e % 2
    rows = a_hbm.shape[0]
    depth = a_hbm.shape[1] // 4
    taps = f_hbm.shape[1]

    def flip(bit, by):
        return 1 - bit if by else bit

    def at(xl_, core_, y_, xh_, z_):
        return {"basis": xl_ * 2 + core_, "tm": (y_ * 2 + xh_) * NZ + z_}

    def remote(src, dst, send, recv, where):
        return pltpu.make_async_remote_copy(
            src_ref=src, dst_ref=dst, send_sem=send, recv_sem=recv,
            device_id=where, device_id_type=MESH,
        )

    peers = []
    for k in range(4):
        for dc in range(2):
            if k or dc:
                peers.append(at(flip(xl, k & 1), flip(core, dc), y, flip(xh, k >> 1), z))
    for dy in range(1, NY):
        for dx in range(2):
            peers.append(at(xl, core, (y + dy) % NY, flip(xh, dx), z))
    for dz in range(1, NZ):
        peers.append(at(xl, core, y, xh, (z + dz) % NZ))
    barrier = pltpu.get_barrier_semaphore()
    for where in peers:
        pl.semaphore_signal(barrier, inc=1, device_id=where, device_id_type=MESH)

    load_f = pltpu.make_async_copy(f_hbm, filt, local_sem.at[0])
    load_f.start()
    keep_a = pltpu.make_async_copy(
        a_hbm.at[:, pl.ds(pl.multiple_of(i * depth, LANES), depth)], a_all.at[z, 0, core], local_sem.at[1]
    )
    keep_a.start()
    keep_s = pltpu.make_async_copy(s_ref, s1.at[e], local_sem.at[2])
    keep_s.start()
    s_all[:, 2 * NY] = jnp.zeros((NZ,) + s_ref.shape, BF)
    pl.semaphore_wait(barrier, len(peers))

    pending = []
    for dy in range(NY):
        for dx in range(2):
            if dy or dx:
                c = remote(s_ref, s1.at[e], s1_send.at[dy * 2 + dx], s1_recv.at[dy * 2 + dx],
                           at(xl, core, (y + dy) % NY, flip(xh, dx), z))
                c.start()
                pending.append(c)
    for k in range(4):
        for dc in range(2):
            if k or dc:
                txl, tcore, txh = flip(xl, k & 1), flip(core, dc), flip(xh, k >> 1)
                c = remote(
                    a_hbm.at[:, pl.ds(pl.multiple_of((txl * 2 + tcore) * depth, LANES), depth)],
                    a_all.at[z, k, core], row_send.at[k * 2 + dc], row_recv.at[k * 2 + dc],
                    at(txl, tcore, y, txh, z))
                c.start()
                pending.append(c)
    keep_s.wait()
    for dy in range(NY):
        for dx in range(2):
            if dy or dx:
                src_e = ((y + NY - dy) % NY) * 2 + flip(xh, dx)
                remote(s_ref, s1.at[src_e], s1_send.at[dy * 2 + dx], s1_recv.at[dy * 2 + dx],
                       at(xl, core, y, xh, z)).wait_recv()
    keep_s2 = pltpu.make_async_copy(s1, s_all.at[z, pl.ds(0, 2 * NY)], local_sem.at[3])
    keep_s2.start()
    for dz in range(1, NZ):
        c = remote(s1, s_all.at[z, pl.ds(0, 2 * NY)], s2_send.at[dz], s2_recv.at[dz],
                   at(xl, core, y, xh, (z + dz) % NZ))
        c.start()
        pending.append(c)

    def ring(way, hop, k):
        src_z = (z + (NZ - hop if way == 0 else hop)) % NZ
        to_z = (z + (1 if way == 0 else NZ - 1)) % NZ
        return remote(a_all.at[src_z, k], a_all.at[src_z, k], ring_send.at[way, hop, k],
                      ring_recv.at[way, hop, k], at(xl, core, y, xh, to_z))

    def arrive(way, hop, k):
        src_z = (z + (NZ - 1 - hop if way == 0 else hop + 1)) % NZ
        remote(a_all.at[src_z, k], a_all.at[src_z, k], ring_send.at[way, hop, k],
               ring_recv.at[way, hop, k], at(xl, core, y, xh, z)).wait_recv()

    def carries(way, hop, k):
        return hop < 3 or (k < 2) == (way == 0)

    def launch(way, hop, k):
        c = ring(way, hop, k)
        c.start()
        pending.append(c)

    keep_a.wait()
    for k in range(4):
        for dc in range(2):
            if k or dc:
                remote(
                    a_hbm.at[:, pl.ds(0, depth)],
                    a_all.at[z, k, flip(core, dc)], row_send.at[k * 2 + dc], row_recv.at[k * 2 + dc],
                    at(xl, core, y, xh, z)).wait_recv()
        for way in range(2):
            launch(way, 0, k)

    def event(dist, k):
        for way in range(2):
            if carries(way, dist - 1, k):
                arrive(way, dist - 1, k)
                if dist < 4 and carries(way, dist, k):
                    launch(way, dist, k)

    keep_s2.wait()
    for dz in range(1, NZ):
        remote(s1, s_all.at[(z + NZ - dz) % NZ, pl.ds(0, 2 * NY)], s2_send.at[dz], s2_recv.at[dz],
               at(xl, core, y, xh, z)).wait_recv()
    load_f.wait()

    width = 3 * LANES

    def hankel(pair):
        for yy in range(2):
            base = ((2 * pair + yy) * 2 + xh) * NZ + z
            blocks = []
            for q in range(5):
                b = base + q
                blocks.append(s_all[b % NZ, b // NZ].astype(F32))
            strip = jnp.concatenate(blocks, axis=1)
            span = strip.shape[1]
            for s in range(STRIDE):
                moved = strip if s == 0 else pltpu.roll(strip, span - s, 1)
                for d in range(3):
                    expand[d * 16 + s * STRIDE:d * 16 + (s + 1) * STRIDE, :] = moved[d * STRIDE:(d + 1) * STRIDE, :]

            def one(b, carry):
                turned = pltpu.roll(expand[...], lax.rem(span - STRIDE * b, span), 1).astype(BF)
                for part in range(taps // (16 * 32)):
                    for d in range(3):
                        hank[pl.ds(pl.multiple_of((32 * part + b) * 16, 16), 16),
                             yy * width + d * LANES:yy * width + (d + 1) * LANES] = (
                            turned[d * 16:(d + 1) * 16, part * LANES:(part + 1) * LANES])
                return carry

            lax.fori_loop(0, 32, one, 0)

    def correlate(pair, nb):
        def one(mb, carry):
            r = pl.ds(pl.multiple_of(mb * 512, 512), 512)
            corr[r, pair * 768 + nb * 256:pair * 768 + (nb + 1) * 256] = jnp.dot(
                filt[r, :], hank[:, nb * 256:(nb + 1) * 256], preferred_element_type=F32).astype(BF)
            return carry

        lax.fori_loop(0, filt.shape[0] // 512, one, 0)

    def pieces(t):
        if t == 0:
            return [(z, 0), (z, 2)], [(z, 1), (z, 3)]
        if t == 7:
            far = (z + 4) % NZ
            return [(far, 0), (far, 2)], [(far, 1), (far, 3)]
        dist, kp = (t + 1) // 2, (t + 1) % 2
        lo, hi = (z + NZ - dist) % NZ, (z + dist) % NZ
        return [(lo, 2 * kp), (hi, 2 * kp)], [(lo, 2 * kp + 1), (hi, 2 * kp + 1)]

    def project(t):
        keep, give = pieces(t)
        left = jnp.concatenate(
            [a_all[zs, k, c] for c in (1 - core, core) for zs, k in keep + give], axis=0)

        def one(nb, carry):
            cols = pl.ds(pl.multiple_of(nb * 256, 256), 256)
            part = jnp.dot(left, corr[:, cols], preferred_element_type=F32)
            c1s[t, :, cols] = part[:128].astype(BF)
            own[t, :, cols] = part[128:]
            return carry

        lax.fori_loop(0, corr.shape[1] // 256, one, 0)
        c = remote(c1s.at[t], c1r.at[t], c1_send.at[t], c1_recv.at[t], at(xl, 1 - core, y, xh, z))
        c.start()
        pending.append(c)

    def halve(t):
        remote(c1s.at[t], c1r.at[t], c1_send.at[t], c1_recv.at[t], at(xl, core, y, xh, z)).wait_recv()
        c2s[t] = (own[t, 64:128] + c1r[t, 64:128].astype(F32)).astype(BF)
        c = remote(c2s.at[t], c2r.at[t], c2_send.at[t], c2_recv.at[t], at(1 - xl, core, y, xh, z))
        c.start()
        pending.append(c)
        own[t, 0:64] = own[t, 0:64] + c1r[t, 0:64].astype(F32)

    def out_rows(t, sub, y_src):
        zs, k = pieces(t)[0][sub]
        return pl.ds(pl.multiple_of(((y_src * 2 + flip(xh, k >> 1)) * NZ + zs) * rows, rows), rows)

    def finish(t):
        remote(c2s.at[t], c2r.at[t], c2_send.at[t], c2_recv.at[t], at(xl, core, y, xh, z)).wait_recv()
        done[t] = (own[t, 0:64] + c2r[t].astype(F32)).astype(BF)
        for sub in range(2):
            for dy in range(NY):
                to_y = (y + dy) % NY
                src = done.at[t, pl.ds(sub * rows, rows), pl.ds(pl.multiple_of(to_y * width, LANES), width)]
                dst = out_ref.at[out_rows(t, sub, y)]
                n = (t * 2 + sub) * NY + dy
                if dy == 0:
                    c = pltpu.make_async_copy(src, dst, keep_sem.at[t * 2 + sub])
                    c.start()
                    kept.append(c)
                else:
                    c = remote(src, dst, c3_send.at[n], c3_recv.at[n], at(xl, core, to_y, xh, z))
                    c.start()
                    pending.append(c)

    kept = []
    hankel(0)
    event(1, 0)
    correlate(0, 0)
    correlate(0, 1)
    event(1, 1)
    correlate(0, 2)
    hankel(1)
    event(1, 2)
    correlate(1, 0)
    correlate(1, 1)
    event(1, 3)
    correlate(1, 2)
    project(0)
    event(2, 0)
    project(1)
    halve(0)
    project(2)
    event(2, 1)
    halve(1)
    project(3)
    halve(2)
    event(2, 2)
    finish(0)
    halve(3)
    event(2, 3)
    project(4)
    event(3, 0)
    halve(4)
    finish(1)
    event(3, 1)
    project(5)
    event(3, 2)
    halve(5)
    finish(2)
    event(3, 3)
    project(6)
    event(4, 0)
    event(4, 2)
    halve(6)
    finish(3)
    event(4, 1)
    event(4, 3)
    project(7)
    finish(4)
    halve(7)
    finish(5)
    finish(6)
    finish(7)

    for t in range(8):
        for sub in range(2):
            for dy in range(1, NY):
                n = (t * 2 + sub) * NY + dy
                src_y = (y + NY - dy) % NY
                remote(done.at[t, pl.ds(sub * rows, rows), pl.ds(0, width)], out_ref.at[out_rows(t, sub, src_y)],
                       c3_send.at[n], c3_recv.at[n], at(xl, core, y, xh, z)).wait_recv()
    for c in pending:
        c.wait_send()
    for c in kept:
        c.wait()


def shards(strain, basis_filters, coefficients):
    detectors, block_len = strain.shape
    filters_here, taps = basis_filters.shape
    rows, _ = coefficients.shape
    phases = strain.reshape(detectors, block_len // STRIDE, STRIDE).transpose(0, 2, 1)
    phases = jnp.pad(phases.reshape(detectors * STRIDE, block_len // STRIDE), ((0, 16 - detectors * STRIDE), (0, 0)))
    width = detectors * LANES
    cols = NY * width
    out_rows = rows * 64
    dma = pltpu.SemaphoreType.DMA
    out = pl.pallas_call(
        kernel,
        out_shape=jax.ShapeDtypeStruct((out_rows, width), BF),
        in_specs=[
            pl.BlockSpec(memory_space=pltpu.VMEM),
            pl.BlockSpec(memory_space=pl.ANY),
            pl.BlockSpec(memory_space=pl.ANY),
        ],
        out_specs=pl.BlockSpec(memory_space=pltpu.VMEM),
        scratch_shapes=[
            pltpu.VMEM((NZ, 4, 2, rows, filters_here), BF),
            pltpu.VMEM((2 * NY, 16, LANES), BF),
            pltpu.VMEM((NZ, 2 * NY + 1, 16, LANES), BF),
            pltpu.VMEM((filters_here, taps), BF),
            pltpu.VMEM((taps, 2 * width), BF),
            pltpu.VMEM((48, 5 * LANES), F32),
            pltpu.VMEM((filters_here, cols), BF),
            pltpu.VMEM((8, 128, cols), BF),
            pltpu.VMEM((8, 128, cols), BF),
            pltpu.VMEM((8, 128, cols), F32),
            pltpu.VMEM((8, 64, cols), BF),
            pltpu.VMEM((8, 64, cols), BF),
            pltpu.VMEM((8, 64, cols), BF),
            dma((4,)),
            dma((8,)), dma((8,)), dma((8,)), dma((8,)), dma((8,)), dma((8,)),
            dma((2, 4, 4)), dma((2, 4, 4)),
            dma((8,)), dma((8,)), dma((8,)), dma((8,)),
            dma((64,)), dma((64,)), dma((16,)),
        ],
        compiler_params=pltpu.CompilerParams(
            collective_id=0, has_side_effects=True, vmem_limit_bytes=60 * 1024 * 1024),
    )(phases, basis_filters, coefficients)
    return out.reshape(out_rows, detectors, LANES)


def solution(mesh):
    placed = (P(None, "tm"), P("basis", None), P(("basis", "tm"), None))
    return jax.shard_map(
        shards, mesh=mesh, in_specs=placed, out_specs=P("basis", None, "tm"), check_vma=False
    )
```

```python
import jax
import jax.numpy as jnp
from jax import lax
from jax.experimental import pallas as pl
from jax.experimental.pallas import tpu as pltpu
from jax.sharding import PartitionSpec as P

MESH = pl.DeviceIdType.MESH
STRIDE = 4
NZ, NY = 8, 4
LANES = 128
BF, F32 = jnp.bfloat16, jnp.float32


def kernel(
    s_ref, f_hbm, a_hbm, out_ref,
    a_all, s1, s_next, filt, hank, expand, corr, c1s, c1r, own, c2s, c2r, done,
    local_sem, s1_send, s1_recv, s2_send, s2_recv, row_send, row_recv,
    ring_send, ring_recv, c1_send, c1_recv, c2_send, c2_recv, c3_send, c3_recv, keep_sem,
):
    i = lax.axis_index("basis")
    j = lax.axis_index("tm")
    xl, core = i // 2, i % 2
    e, z = j // NZ, j % NZ
    y, xh = e // 2, e % 2
    rows = a_hbm.shape[0]
    depth = a_hbm.shape[1] // 4
    taps = f_hbm.shape[1]

    def flip(bit, by):
        return 1 - bit if by else bit

    def at(xl_, core_, y_, xh_, z_):
        return {"basis": xl_ * 2 + core_, "tm": (y_ * 2 + xh_) * NZ + z_}

    def remote(src, dst, send, recv, where):
        return pltpu.make_async_remote_copy(
            src_ref=src, dst_ref=dst, send_sem=send, recv_sem=recv,
            device_id=where, device_id_type=MESH,
        )

    peers = []
    for k in range(4):
        for dc in range(2):
            if k or dc:
                peers.append(at(flip(xl, k & 1), flip(core, dc), y, flip(xh, k >> 1), z))
    for dy in range(1, NY):
        for dx in range(2):
            peers.append(at(xl, core, (y + dy) % NY, flip(xh, dx), z))
    for dz in range(1, NZ):
        peers.append(at(xl, core, y, xh, (z + dz) % NZ))
    barrier = pltpu.get_barrier_semaphore()
    for where in peers:
        pl.semaphore_signal(barrier, inc=1, device_id=where, device_id_type=MESH)

    load_f = pltpu.make_async_copy(f_hbm, filt, local_sem.at[0])
    load_f.start()
    keep_a = pltpu.make_async_copy(
        a_hbm.at[:, pl.ds(pl.multiple_of(i * depth, LANES), depth)], a_all.at[z, 0, core], local_sem.at[1]
    )
    keep_a.start()
    keep_s = pltpu.make_async_copy(s_ref, s1.at[y, xh], local_sem.at[2])
    keep_s.start()
    s1[NY] = jnp.zeros((2,) + s_ref.shape, BF)
    pl.semaphore_wait(barrier, len(peers))

    pending = []
    for dy in range(NY):
        for dx in range(2):
            if dy or dx:
                c = remote(s_ref, s1.at[y, xh], s1_send.at[dy * 2 + dx], s1_recv.at[dy * 2 + dx],
                           at(xl, core, (y + dy) % NY, flip(xh, dx), z))
                c.start()
                pending.append(c)
    for k in range(4):
        for dc in range(2):
            if k or dc:
                txl, tcore, txh = flip(xl, k & 1), flip(core, dc), flip(xh, k >> 1)
                c = remote(
                    a_hbm.at[:, pl.ds(pl.multiple_of((txl * 2 + tcore) * depth, LANES), depth)],
                    a_all.at[z, k, core], row_send.at[k * 2 + dc], row_recv.at[k * 2 + dc],
                    at(txl, tcore, y, txh, z))
                c.start()
                pending.append(c)
    def ring(way, hop, k):
        src_z = (z + (NZ - hop if way == 0 else hop)) % NZ
        to_z = (z + (1 if way == 0 else NZ - 1)) % NZ
        return remote(a_all.at[src_z, k], a_all.at[src_z, k], ring_send.at[way, hop, k],
                      ring_recv.at[way, hop, k], at(xl, core, y, xh, to_z))

    def arrive(way, hop, k):
        src_z = (z + (NZ - 1 - hop if way == 0 else hop + 1)) % NZ
        remote(a_all.at[src_z, k], a_all.at[src_z, k], ring_send.at[way, hop, k],
               ring_recv.at[way, hop, k], at(xl, core, y, xh, z)).wait_recv()

    def carries(way, hop, k):
        return hop < 3 or (k < 2) == (way == 0)

    def launch(way, hop, k):
        c = ring(way, hop, k)
        c.start()
        pending.append(c)

    keep_a.wait()
    for k in range(4):
        for dc in range(2):
            if k or dc:
                remote(
                    a_hbm.at[:, pl.ds(0, depth)],
                    a_all.at[z, k, flip(core, dc)], row_send.at[k * 2 + dc], row_recv.at[k * 2 + dc],
                    at(xl, core, y, xh, z)).wait_recv()
        for way in range(2):
            launch(way, 0, k)
        if k == 0:
            keep_s.wait()
            for dy in range(NY):
                for dx in range(2):
                    if dy or dx:
                        remote(s_ref, s1.at[(y + NY - dy) % NY, flip(xh, dx)], s1_send.at[dy * 2 + dx],
                               s1_recv.at[dy * 2 + dx], at(xl, core, y, xh, z)).wait_recv()
            for q in range(1, 5):
                m = xh + (NZ + q - 1 - z) // NZ
                c = remote(s1.at[pl.ds(m // 2, NY), m % 2], s_next.at[q - 1], s2_send.at[q], s2_recv.at[q],
                           at(xl, core, y, xh, (z + NZ - q) % NZ))
                c.start()
                pending.append(c)

    def event(dist, k):
        for way in range(2):
            if carries(way, dist - 1, k):
                arrive(way, dist - 1, k)
                if dist < 4 and carries(way, dist, k):
                    launch(way, dist, k)

    event(1, 0)
    for q in range(1, 5):
        remote(s1.at[pl.ds(0, NY), 0], s_next.at[q - 1], s2_send.at[q], s2_recv.at[q],
               at(xl, core, y, xh, z)).wait_recv()
    event(1, 1)
    load_f.wait()

    width = 3 * LANES

    def hankel(pair):
        for yy in range(2):
            ya = (y + 2 * pair + yy) % NY
            blocks = [s1[ya, xh].astype(F32)]
            for q in range(4):
                blocks.append(s_next[q, ya].astype(F32))
            strip = jnp.concatenate(blocks, axis=1)
            span = strip.shape[1]
            for s in range(STRIDE):
                moved = strip if s == 0 else pltpu.roll(strip, span - s, 1)
                for d in range(3):
                    expand[d * 16 + s * STRIDE:d * 16 + (s + 1) * STRIDE, :] = moved[d * STRIDE:(d + 1) * STRIDE, :]

            def one(b, carry):
                turned = pltpu.roll(expand[...], lax.rem(span - STRIDE * b, span), 1).astype(BF)
                for part in range(taps // (16 * 32)):
                    for d in range(3):
                        hank[pl.ds(pl.multiple_of((32 * part + b) * 16, 16), 16),
                             yy * width + d * LANES:yy * width + (d + 1) * LANES] = (
                            turned[d * 16:(d + 1) * 16, part * LANES:(part + 1) * LANES])
                return carry

            lax.fori_loop(0, 32, one, 0)

    def correlate(pair, nb):
        def one(mb, carry):
            r = pl.ds(pl.multiple_of(mb * 512, 512), 512)
            corr[r, pair * 768 + nb * 256:pair * 768 + (nb + 1) * 256] = jnp.dot(
                filt[r, :], hank[:, nb * 256:(nb + 1) * 256], preferred_element_type=F32).astype(BF)
            return carry

        lax.fori_loop(0, filt.shape[0] // 512, one, 0)

    def pieces(t):
        if t == 0:
            return [(z, 0), (z, 2)], [(z, 1), (z, 3)]
        if t == 7:
            far = (z + 4) % NZ
            return [(far, 0), (far, 2)], [(far, 1), (far, 3)]
        dist, kp = (t + 1) // 2, (t + 1) % 2
        lo, hi = (z + NZ - dist) % NZ, (z + dist) % NZ
        return [(lo, 2 * kp), (hi, 2 * kp)], [(lo, 2 * kp + 1), (hi, 2 * kp + 1)]

    half = 2 * width

    def span_of(p):
        return pl.ds(p * half, half)

    def first(t, p):
        u = t * 2 + p
        cut = (t, slice(None), span_of(p))
        return remote(c1s.at[cut], c1r.at[cut], c1_send.at[u], c1_recv.at[u], at(xl, 1 - core, y, xh, z))

    def second(t, p):
        u = t * 2 + p
        cut = (t, slice(None), span_of(p))
        return remote(c2s.at[cut], c2r.at[cut], c2_send.at[u], c2_recv.at[u], at(1 - xl, core, y, xh, z))

    def project(t, p):
        keep, give = pieces(t)
        left = jnp.concatenate(
            [a_all[zs, k, c] for c in (1 - core, core) for zs, k in keep + give], axis=0)

        def one(nb, carry):
            cols = pl.ds(pl.multiple_of(p * half + nb * 256, 256), 256)
            part = jnp.dot(left, corr[:, cols], preferred_element_type=F32)
            c1s[t, :, cols] = part[:128].astype(BF)
            own[t, :, cols] = part[128:]
            return carry

        lax.fori_loop(0, half // 256, one, 0)
        c = first(t, p)
        c.start()
        pending.append(c)

    def halve(t, p):
        first(t, p).wait_recv()
        cols = span_of(p)
        c2s[t, :, cols] = (own[t, 64:128, cols] + c1r[t, 64:128, cols].astype(F32)).astype(BF)
        c = second(t, p)
        c.start()
        pending.append(c)
        own[t, 0:64, cols] = own[t, 0:64, cols] + c1r[t, 0:64, cols].astype(F32)

    def out_rows(t, sub, y_src):
        zs, k = pieces(t)[0][sub]
        return pl.ds(pl.multiple_of(((y_src * 2 + flip(xh, k >> 1)) * NZ + zs) * rows, rows), rows)

    def finish(t, p):
        second(t, p).wait_recv()
        cols = span_of(p)
        done[t, :, cols] = (own[t, 0:64, cols] + c2r[t, :, cols].astype(F32)).astype(BF)
        for sub in range(2):
            for dy in (2 * p, 2 * p + 1):
                src = done.at[t, pl.ds(sub * rows, rows), pl.ds(dy * width, width)]
                dst = out_ref.at[out_rows(t, sub, y)]
                n = (t * 2 + sub) * NY + dy
                if dy == 0:
                    c = pltpu.make_async_copy(src, dst, keep_sem.at[t * 2 + sub])
                    c.start()
                    kept.append(c)
                else:
                    c = remote(src, dst, c3_send.at[n], c3_recv.at[n], at(xl, core, (y + dy) % NY, xh, z))
                    c.start()
                    pending.append(c)

    kept = []
    hankel(1)
    event(1, 2)
    event(1, 3)
    correlate(1, 0)
    event(2, 0)
    correlate(1, 1)
    event(2, 1)
    correlate(1, 2)
    project(0, 1)
    project(1, 1)
    halve(0, 1)
    event(2, 2)
    project(2, 1)
    halve(1, 1)
    project(3, 1)
    halve(2, 1)
    event(2, 3)
    project(4, 1)
    halve(3, 1)
    hankel(0)
    halve(4, 1)
    event(3, 0)
    event(3, 1)
    finish(0, 1)
    correlate(0, 0)
    event(3, 2)
    project(5, 1)
    finish(1, 1)
    correlate(0, 1)
    halve(5, 1)
    event(3, 3)
    finish(2, 1)
    project(6, 1)
    correlate(0, 2)
    halve(6, 1)
    finish(3, 1)
    project(0, 0)
    project(1, 0)
    halve(0, 0)
    finish(4, 1)
    project(2, 0)
    halve(1, 0)
    project(3, 0)
    halve(2, 0)
    finish(5, 1)
    for k in range(4):
        event(4, k)
    project(7, 1)
    halve(3, 0)
    project(4, 0)
    halve(7, 1)
    finish(6, 1)
    project(5, 0)
    halve(4, 0)
    finish(0, 0)
    project(6, 0)
    halve(5, 0)
    finish(1, 0)
    project(7, 0)
    halve(6, 0)
    finish(2, 0)
    halve(7, 0)
    finish(3, 0)
    finish(7, 1)
    for t in range(4, 8):
        finish(t, 0)

    for t in range(8):
        for sub in range(2):
            for dy in range(1, NY):
                n = (t * 2 + sub) * NY + dy
                src_y = (y + NY - dy) % NY
                remote(done.at[t, pl.ds(sub * rows, rows), pl.ds(0, width)], out_ref.at[out_rows(t, sub, src_y)],
                       c3_send.at[n], c3_recv.at[n], at(xl, core, y, xh, z)).wait_recv()
    for c in pending:
        c.wait_send()
    for c in kept:
        c.wait()


def shards(strain, basis_filters, coefficients):
    detectors, block_len = strain.shape
    filters_here, taps = basis_filters.shape
    rows, _ = coefficients.shape
    phases = strain.reshape(detectors, block_len // STRIDE, STRIDE).transpose(0, 2, 1)
    phases = jnp.pad(phases.reshape(detectors * STRIDE, block_len // STRIDE), ((0, 16 - detectors * STRIDE), (0, 0)))
    width = detectors * LANES
    cols = NY * width
    out_rows = rows * 64
    dma = pltpu.SemaphoreType.DMA
    out = pl.pallas_call(
        kernel,
        out_shape=jax.ShapeDtypeStruct((out_rows, width), BF),
        in_specs=[
            pl.BlockSpec(memory_space=pltpu.VMEM),
            pl.BlockSpec(memory_space=pl.ANY),
            pl.BlockSpec(memory_space=pl.ANY),
        ],
        out_specs=pl.BlockSpec(memory_space=pltpu.VMEM),
        scratch_shapes=[
            pltpu.VMEM((NZ, 4, 2, rows, filters_here), BF),
            pltpu.VMEM((NY + 1, 2, 16, LANES), BF),
            pltpu.VMEM((4, NY, 16, LANES), BF),
            pltpu.VMEM((filters_here, taps), BF),
            pltpu.VMEM((taps, 2 * width), BF),
            pltpu.VMEM((48, 5 * LANES), F32),
            pltpu.VMEM((filters_here, cols), BF),
            pltpu.VMEM((8, 128, cols), BF),
            pltpu.VMEM((8, 128, cols), BF),
            pltpu.VMEM((8, 128, cols), F32),
            pltpu.VMEM((8, 64, cols), BF),
            pltpu.VMEM((8, 64, cols), BF),
            pltpu.VMEM((8, 64, cols), BF),
            dma((4,)),
            dma((8,)), dma((8,)), dma((8,)), dma((8,)), dma((8,)), dma((8,)),
            dma((2, 4, 4)), dma((2, 4, 4)),
            dma((16,)), dma((16,)), dma((16,)), dma((16,)),
            dma((64,)), dma((64,)), dma((16,)),
        ],
        compiler_params=pltpu.CompilerParams(
            collective_id=0, has_side_effects=True, vmem_limit_bytes=60 * 1024 * 1024),
    )(phases, basis_filters, coefficients)
    return out.reshape(out_rows, detectors, LANES)


def solution(mesh):
    placed = (P(None, "tm"), P("basis", None), P(("basis", "tm"), None))
    return jax.shard_map(
        shards, mesh=mesh, in_specs=placed, out_specs=P("basis", None, "tm"), check_vma=False
    )
```

```python
import jax
import jax.numpy as jnp
from jax import lax
from jax.experimental import pallas as pl
from jax.experimental.pallas import tpu as pltpu
from jax.sharding import PartitionSpec as P

MESH = pl.DeviceIdType.MESH
STRIDE = 4
NZ, NY = 8, 4
LANES = 128
BF, F32 = jnp.bfloat16, jnp.float32


def kernel(
    s_ref, f_hbm, a_hbm, out_ref,
    a_all, s1, s_next, filt, hank, expand, corr, c1s, c1r, own, c2s, c2r, done,
    local_sem, s1_send, s1_recv, s2_send, s2_recv, row_send, row_recv,
    ring_send, ring_recv, c1_send, c1_recv, c2_send, c2_recv, c3_send, c3_recv, keep_sem,
):
    i = lax.axis_index("basis")
    j = lax.axis_index("tm")
    xl, core = i // 2, i % 2
    e, z = j // NZ, j % NZ
    y, xh = e // 2, e % 2
    rows = a_hbm.shape[0]
    depth = a_hbm.shape[1] // 4
    taps = f_hbm.shape[1]

    def flip(bit, by):
        return 1 - bit if by else bit

    def at(xl_, core_, y_, xh_, z_):
        return {"basis": xl_ * 2 + core_, "tm": (y_ * 2 + xh_) * NZ + z_}

    def remote(src, dst, send, recv, where):
        return pltpu.make_async_remote_copy(
            src_ref=src, dst_ref=dst, send_sem=send, recv_sem=recv,
            device_id=where, device_id_type=MESH,
        )

    peers = []
    for k in range(4):
        for dc in range(2):
            if k or dc:
                peers.append(at(flip(xl, k & 1), flip(core, dc), y, flip(xh, k >> 1), z))
    for dy in range(1, NY):
        for dx in range(2):
            peers.append(at(xl, core, (y + dy) % NY, flip(xh, dx), z))
    for dz in range(1, NZ):
        peers.append(at(xl, core, y, xh, (z + dz) % NZ))
    barrier = pltpu.get_barrier_semaphore()
    for where in peers:
        pl.semaphore_signal(barrier, inc=1, device_id=where, device_id_type=MESH)

    load_f = pltpu.make_async_copy(f_hbm, filt, local_sem.at[0])
    load_f.start()
    keep_a = pltpu.make_async_copy(
        a_hbm.at[:, pl.ds(pl.multiple_of(i * depth, LANES), depth)], a_all.at[z, 0, core], local_sem.at[1]
    )
    keep_a.start()
    keep_s = pltpu.make_async_copy(s_ref, s1.at[y, xh], local_sem.at[2])
    keep_s.start()
    s1[NY] = jnp.zeros((2,) + s_ref.shape, BF)
    pl.semaphore_wait(barrier, len(peers))

    pending = []
    for dy in range(NY):
        for dx in range(2):
            if dy or dx:
                c = remote(s_ref, s1.at[y, xh], s1_send.at[dy * 2 + dx], s1_recv.at[dy * 2 + dx],
                           at(xl, core, (y + dy) % NY, flip(xh, dx), z))
                c.start()
                pending.append(c)
    for k in range(4):
        for dc in range(2):
            if k or dc:
                txl, tcore, txh = flip(xl, k & 1), flip(core, dc), flip(xh, k >> 1)
                c = remote(
                    a_hbm.at[:, pl.ds(pl.multiple_of((txl * 2 + tcore) * depth, LANES), depth)],
                    a_all.at[z, k, core], row_send.at[k * 2 + dc], row_recv.at[k * 2 + dc],
                    at(txl, tcore, y, txh, z))
                c.start()
                pending.append(c)
    def ring(way, hop, k):
        src_z = (z + (NZ - hop if way == 0 else hop)) % NZ
        to_z = (z + (1 if way == 0 else NZ - 1)) % NZ
        return remote(a_all.at[src_z, k], a_all.at[src_z, k], ring_send.at[way, hop, k],
                      ring_recv.at[way, hop, k], at(xl, core, y, xh, to_z))

    def arrive(way, hop, k):
        src_z = (z + (NZ - 1 - hop if way == 0 else hop + 1)) % NZ
        remote(a_all.at[src_z, k], a_all.at[src_z, k], ring_send.at[way, hop, k],
               ring_recv.at[way, hop, k], at(xl, core, y, xh, z)).wait_recv()

    def carries(way, hop, k):
        return hop < 3 or (k < 2) == (way == 0)

    def launch(way, hop, k):
        c = ring(way, hop, k)
        c.start()
        pending.append(c)

    keep_a.wait()
    for k in range(4):
        for dc in range(2):
            if k or dc:
                remote(
                    a_hbm.at[:, pl.ds(0, depth)],
                    a_all.at[z, k, flip(core, dc)], row_send.at[k * 2 + dc], row_recv.at[k * 2 + dc],
                    at(xl, core, y, xh, z)).wait_recv()
        for way in range(2):
            launch(way, 0, k)
        if k == 0:
            keep_s.wait()
            for dy in range(NY):
                for dx in range(2):
                    if dy or dx:
                        remote(s_ref, s1.at[(y + NY - dy) % NY, flip(xh, dx)], s1_send.at[dy * 2 + dx],
                               s1_recv.at[dy * 2 + dx], at(xl, core, y, xh, z)).wait_recv()
            for q in range(1, 5):
                m = xh + (NZ + q - 1 - z) // NZ
                c = remote(s1.at[pl.ds(m // 2, NY), m % 2], s_next.at[q - 1], s2_send.at[q], s2_recv.at[q],
                           at(xl, core, y, xh, (z + NZ - q) % NZ))
                c.start()
                pending.append(c)

    def event(dist, k):
        for way in range(2):
            if carries(way, dist - 1, k):
                arrive(way, dist - 1, k)
                if dist < 4 and carries(way, dist, k):
                    launch(way, dist, k)

    event(1, 0)
    for q in range(1, 5):
        remote(s1.at[pl.ds(0, NY), 0], s_next.at[q - 1], s2_send.at[q], s2_recv.at[q],
               at(xl, core, y, xh, z)).wait_recv()
    event(1, 1)
    load_f.wait()

    width = 3 * LANES

    def hankel(pair):
        for yy in range(2):
            ya = (y + 2 * pair + yy) % NY
            blocks = [s1[ya, xh].astype(F32)]
            for q in range(4):
                blocks.append(s_next[q, ya].astype(F32))
            strip = jnp.concatenate(blocks, axis=1)
            span = strip.shape[1]
            for s in range(STRIDE):
                moved = strip if s == 0 else pltpu.roll(strip, span - s, 1)
                for d in range(3):
                    expand[d * 16 + s * STRIDE:d * 16 + (s + 1) * STRIDE, :] = moved[d * STRIDE:(d + 1) * STRIDE, :]

            def one(g, moving):
                for b in range(4):
                    turned = (moving if b == 0 else pltpu.roll(moving, span - STRIDE * b, 1)).astype(BF)
                    for part in range(taps // (16 * 32)):
                        for d in range(3):
                            hank[pl.ds(pl.multiple_of((32 * part + 4 * g + b) * 16, 16), 16),
                                 yy * width + d * LANES:yy * width + (d + 1) * LANES] = (
                                turned[d * 16:(d + 1) * 16, part * LANES:(part + 1) * LANES])
                return pltpu.roll(moving, span - 4 * STRIDE, 1)

            lax.fori_loop(0, 8, one, expand[...])

    def correlate(pair, nb):
        def one(mb, carry):
            r = pl.ds(pl.multiple_of(mb * 512, 512), 512)
            corr[r, pair * 768 + nb * 256:pair * 768 + (nb + 1) * 256] = jnp.dot(
                filt[r, :], hank[:, nb * 256:(nb + 1) * 256], preferred_element_type=F32).astype(BF)
            return carry

        lax.fori_loop(0, filt.shape[0] // 512, one, 0)

    def pieces(t):
        if t == 0:
            return [(z, 0), (z, 2)], [(z, 1), (z, 3)]
        if t == 7:
            far = (z + 4) % NZ
            return [(far, 0), (far, 2)], [(far, 1), (far, 3)]
        dist, kp = (t + 1) // 2, (t + 1) % 2
        lo, hi = (z + NZ - dist) % NZ, (z + dist) % NZ
        return [(lo, 2 * kp), (hi, 2 * kp)], [(lo, 2 * kp + 1), (hi, 2 * kp + 1)]

    half = 2 * width

    def span_of(p):
        return pl.ds(p * half, half)

    def first(t, p):
        u = t * 2 + p
        cut = (t, slice(None), span_of(p))
        return remote(c1s.at[cut], c1r.at[cut], c1_send.at[u], c1_recv.at[u], at(xl, 1 - core, y, xh, z))

    def second(t, p):
        u = t * 2 + p
        cut = (t, slice(None), span_of(p))
        return remote(c2s.at[cut], c2r.at[cut], c2_send.at[u], c2_recv.at[u], at(1 - xl, core, y, xh, z))

    def project(t, p):
        keep, give = pieces(t)
        left = jnp.concatenate(
            [a_all[zs, k, c] for c in (1 - core, core) for zs, k in keep + give], axis=0)

        cols = span_of(p)
        part = jnp.dot(left, corr[:, cols], preferred_element_type=F32)
        c1s[t, :, cols] = part[:128].astype(BF)
        own[t, :, cols] = part[128:]
        c = first(t, p)
        c.start()
        pending.append(c)

    def halve(t, p):
        first(t, p).wait_recv()
        cols = span_of(p)
        c2s[t, :, cols] = (own[t, 64:128, cols] + c1r[t, 64:128, cols].astype(F32)).astype(BF)
        c = second(t, p)
        c.start()
        pending.append(c)
        own[t, 0:64, cols] = own[t, 0:64, cols] + c1r[t, 0:64, cols].astype(F32)

    def out_rows(t, sub, y_src):
        zs, k = pieces(t)[0][sub]
        return pl.ds(pl.multiple_of(((y_src * 2 + flip(xh, k >> 1)) * NZ + zs) * rows, rows), rows)

    def finish(t, p):
        second(t, p).wait_recv()
        for dy in (2 * p, 2 * p + 1):
            for d in range(3):
                at_ = pl.ds(dy * width + d * LANES, LANES)
                done[t, dy, d] = (own[t, 0:64, at_] + c2r[t, :, at_].astype(F32)).astype(BF)
        for sub in range(2):
            for dy in (2 * p, 2 * p + 1):
                src = done.at[t, dy, :, pl.ds(sub * rows, rows)]
                dst = out_ref.at[:, out_rows(t, sub, y)]
                n = (t * 2 + sub) * NY + dy
                if dy == 0:
                    c = pltpu.make_async_copy(src, dst, keep_sem.at[t * 2 + sub])
                    c.start()
                    kept.append(c)
                else:
                    c = remote(src, dst, c3_send.at[n], c3_recv.at[n], at(xl, core, (y + dy) % NY, xh, z))
                    c.start()
                    pending.append(c)

    kept = []
    hankel(1)
    event(1, 2)
    event(1, 3)
    correlate(1, 0)
    event(2, 0)
    correlate(1, 1)
    event(2, 1)
    correlate(1, 2)
    project(0, 1)
    project(1, 1)
    halve(0, 1)
    event(2, 2)
    project(2, 1)
    halve(1, 1)
    project(3, 1)
    halve(2, 1)
    event(2, 3)
    project(4, 1)
    halve(3, 1)
    hankel(0)
    halve(4, 1)
    event(3, 0)
    event(3, 1)
    finish(0, 1)
    correlate(0, 0)
    event(3, 2)
    project(5, 1)
    finish(1, 1)
    correlate(0, 1)
    halve(5, 1)
    event(3, 3)
    finish(2, 1)
    project(6, 1)
    correlate(0, 2)
    halve(6, 1)
    finish(3, 1)
    project(0, 0)
    project(1, 0)
    halve(0, 0)
    finish(4, 1)
    project(2, 0)
    halve(1, 0)
    project(3, 0)
    halve(2, 0)
    finish(5, 1)
    for k in range(4):
        event(4, k)
    project(7, 1)
    halve(3, 0)
    project(4, 0)
    halve(7, 1)
    finish(6, 1)
    project(5, 0)
    halve(4, 0)
    finish(0, 0)
    project(6, 0)
    halve(5, 0)
    finish(1, 0)
    project(7, 0)
    halve(6, 0)
    finish(2, 0)
    halve(7, 0)
    finish(3, 0)
    finish(7, 1)
    for t in range(4, 8):
        finish(t, 0)

    for t in range(8):
        for sub in range(2):
            for dy in range(1, NY):
                n = (t * 2 + sub) * NY + dy
                src_y = (y + NY - dy) % NY
                remote(done.at[t, dy, :, pl.ds(sub * rows, rows)], out_ref.at[:, out_rows(t, sub, src_y)],
                       c3_send.at[n], c3_recv.at[n], at(xl, core, y, xh, z)).wait_recv()
    for c in pending:
        c.wait_send()
    for c in kept:
        c.wait()


def shards(strain, basis_filters, coefficients):
    detectors, block_len = strain.shape
    filters_here, taps = basis_filters.shape
    rows, _ = coefficients.shape
    phases = strain.reshape(detectors, block_len // STRIDE, STRIDE).transpose(0, 2, 1)
    phases = jnp.pad(phases.reshape(detectors * STRIDE, block_len // STRIDE), ((0, 16 - detectors * STRIDE), (0, 0)))
    width = detectors * LANES
    cols = NY * width
    out_rows = rows * 64
    dma = pltpu.SemaphoreType.DMA
    out = pl.pallas_call(
        kernel,
        out_shape=jax.ShapeDtypeStruct((detectors, out_rows, LANES), BF),
        in_specs=[
            pl.BlockSpec(memory_space=pltpu.VMEM),
            pl.BlockSpec(memory_space=pl.ANY),
            pl.BlockSpec(memory_space=pl.ANY),
        ],
        out_specs=pl.BlockSpec(memory_space=pltpu.VMEM),
        scratch_shapes=[
            pltpu.VMEM((NZ, 4, 2, rows, filters_here), BF),
            pltpu.VMEM((NY + 1, 2, 16, LANES), BF),
            pltpu.VMEM((4, NY, 16, LANES), BF),
            pltpu.VMEM((filters_here, taps), BF),
            pltpu.VMEM((taps, 2 * width), BF),
            pltpu.VMEM((48, 5 * LANES), F32),
            pltpu.VMEM((filters_here, cols), BF),
            pltpu.VMEM((8, 128, cols), BF),
            pltpu.VMEM((8, 128, cols), BF),
            pltpu.VMEM((8, 128, cols), F32),
            pltpu.VMEM((8, 64, cols), BF),
            pltpu.VMEM((8, 64, cols), BF),
            pltpu.VMEM((8, NY, detectors, 64, LANES), BF),
            dma((4,)),
            dma((8,)), dma((8,)), dma((8,)), dma((8,)), dma((8,)), dma((8,)),
            dma((2, 4, 4)), dma((2, 4, 4)),
            dma((16,)), dma((16,)), dma((16,)), dma((16,)),
            dma((64,)), dma((64,)), dma((16,)),
        ],
        compiler_params=pltpu.CompilerParams(
            collective_id=0, has_side_effects=True, vmem_limit_bytes=60 * 1024 * 1024),
    )(phases, basis_filters, coefficients)
    return out.transpose(1, 0, 2)


def solution(mesh):
    placed = (P(None, "tm"), P("basis", None), P(("basis", "tm"), None))
    return jax.shard_map(
        shards, mesh=mesh, in_specs=placed, out_specs=P("basis", None, "tm"), check_vma=False
    )
```

```python
import jax
import jax.numpy as jnp
from jax import lax
from jax.experimental import pallas as pl
from jax.experimental.pallas import tpu as pltpu
from jax.sharding import PartitionSpec as P

MESH = pl.DeviceIdType.MESH
STRIDE = 4
NZ, NY = 8, 4
LANES = 128
BF, F32 = jnp.bfloat16, jnp.float32


def kernel(
    s_ref, f_hbm, a_hbm, out_ref,
    a_all, s1, s_next, filt, hank, expand, corr, c1s, c1r, own, c2s, c2r, done,
    local_sem, s1_send, s1_recv, s2_send, s2_recv, row_send, row_recv,
    ring_send, ring_recv, c1_send, c1_recv, c2_send, c2_recv, c3_send, c3_recv, keep_sem,
):
    i = lax.axis_index("basis")
    j = lax.axis_index("tm")
    xl, core = i // 2, i % 2
    e, z = j // NZ, j % NZ
    y, xh = e // 2, e % 2
    rows = a_hbm.shape[0]
    depth = a_hbm.shape[1] // 4
    taps = f_hbm.shape[1]

    def flip(bit, by):
        return 1 - bit if by else bit

    def at(xl_, core_, y_, xh_, z_):
        return {"basis": xl_ * 2 + core_, "tm": (y_ * 2 + xh_) * NZ + z_}

    def remote(src, dst, send, recv, where):
        return pltpu.make_async_remote_copy(
            src_ref=src, dst_ref=dst, send_sem=send, recv_sem=recv,
            device_id=where, device_id_type=MESH,
        )

    peers = []
    for k in range(4):
        for dc in range(2):
            if k or dc:
                peers.append(at(flip(xl, k & 1), flip(core, dc), y, flip(xh, k >> 1), z))
    for dy in range(1, NY):
        for dx in range(2):
            peers.append(at(xl, core, (y + dy) % NY, flip(xh, dx), z))
    for dz in range(1, NZ):
        peers.append(at(xl, core, y, xh, (z + dz) % NZ))
    barrier = pltpu.get_barrier_semaphore()
    for where in peers:
        pl.semaphore_signal(barrier, inc=1, device_id=where, device_id_type=MESH)

    load_f = pltpu.make_async_copy(f_hbm, filt, local_sem.at[0])
    load_f.start()
    keep_a = pltpu.make_async_copy(
        a_hbm.at[:, pl.ds(pl.multiple_of(i * depth, LANES), depth)], a_all.at[z, 0, core], local_sem.at[1]
    )
    keep_a.start()
    keep_s = pltpu.make_async_copy(s_ref, s1.at[y, xh], local_sem.at[2])
    keep_s.start()
    s1[NY] = jnp.zeros((2,) + s_ref.shape, BF)
    pl.semaphore_wait(barrier, len(peers))

    pending = []
    for dy in range(NY):
        for dx in range(2):
            if dy or dx:
                c = remote(s_ref, s1.at[y, xh], s1_send.at[dy * 2 + dx], s1_recv.at[dy * 2 + dx],
                           at(xl, core, (y + dy) % NY, flip(xh, dx), z))
                c.start()
                pending.append(c)
    for k in range(4):
        for dc in range(2):
            if k or dc:
                txl, tcore, txh = flip(xl, k & 1), flip(core, dc), flip(xh, k >> 1)
                c = remote(
                    a_hbm.at[:, pl.ds(pl.multiple_of((txl * 2 + tcore) * depth, LANES), depth)],
                    a_all.at[z, k, core], row_send.at[k * 2 + dc], row_recv.at[k * 2 + dc],
                    at(txl, tcore, y, txh, z))
                c.start()
                pending.append(c)
    def ring(way, hop, k):
        src_z = (z + (NZ - hop if way == 0 else hop)) % NZ
        to_z = (z + (1 if way == 0 else NZ - 1)) % NZ
        return remote(a_all.at[src_z, k], a_all.at[src_z, k], ring_send.at[way, hop, k],
                      ring_recv.at[way, hop, k], at(xl, core, y, xh, to_z))

    def arrive(way, hop, k):
        src_z = (z + (NZ - 1 - hop if way == 0 else hop + 1)) % NZ
        remote(a_all.at[src_z, k], a_all.at[src_z, k], ring_send.at[way, hop, k],
               ring_recv.at[way, hop, k], at(xl, core, y, xh, z)).wait_recv()

    def carries(way, hop, k):
        return hop < 3 or (k < 2) == (way == 0)

    def launch(way, hop, k):
        c = ring(way, hop, k)
        c.start()
        pending.append(c)

    keep_a.wait()
    for k in range(4):
        for dc in range(2):
            if k or dc:
                remote(
                    a_hbm.at[:, pl.ds(0, depth)],
                    a_all.at[z, k, flip(core, dc)], row_send.at[k * 2 + dc], row_recv.at[k * 2 + dc],
                    at(xl, core, y, xh, z)).wait_recv()
        for way in range(2):
            launch(way, 0, k)
        if k == 0:
            keep_s.wait()
            for dy in range(NY):
                for dx in range(2):
                    if dy or dx:
                        remote(s_ref, s1.at[(y + NY - dy) % NY, flip(xh, dx)], s1_send.at[dy * 2 + dx],
                               s1_recv.at[dy * 2 + dx], at(xl, core, y, xh, z)).wait_recv()
            for q in range(1, 5):
                m = xh + (NZ + q - 1 - z) // NZ
                c = remote(s1.at[pl.ds(m // 2, NY), m % 2], s_next.at[q - 1], s2_send.at[q], s2_recv.at[q],
                           at(xl, core, y, xh, (z + NZ - q) % NZ))
                c.start()
                pending.append(c)

    def event(dist, k):
        for way in range(2):
            if carries(way, dist - 1, k):
                arrive(way, dist - 1, k)
                if dist < 4 and carries(way, dist, k):
                    launch(way, dist, k)

    event(1, 0)
    for q in range(1, 5):
        remote(s1.at[pl.ds(0, NY), 0], s_next.at[q - 1], s2_send.at[q], s2_recv.at[q],
               at(xl, core, y, xh, z)).wait_recv()
    event(1, 1)
    load_f.wait()

    width = 3 * LANES

    def hankel(pair):
        for yy in range(2):
            ya = (y + 2 * pair + yy) % NY
            blocks = [s1[ya, xh].astype(F32)]
            for q in range(4):
                blocks.append(s_next[q, ya].astype(F32))
            strip = jnp.concatenate(blocks, axis=1)
            span = strip.shape[1]
            for s in range(STRIDE):
                moved = strip if s == 0 else pltpu.roll(strip, span - s, 1)
                for d in range(3):
                    expand[d * 16 + s * STRIDE:d * 16 + (s + 1) * STRIDE, :] = moved[d * STRIDE:(d + 1) * STRIDE, :]

            def one(g, moving):
                for b in range(4):
                    turned = (moving if b == 0 else pltpu.roll(moving, span - STRIDE * b, 1)).astype(BF)
                    for part in range(taps // (16 * 32)):
                        for d in range(3):
                            hank[pl.ds(pl.multiple_of((32 * part + 4 * g + b) * 16, 16), 16),
                                 yy * width + d * LANES:yy * width + (d + 1) * LANES] = (
                                turned[d * 16:(d + 1) * 16, part * LANES:(part + 1) * LANES])
                return pltpu.roll(moving, span - 4 * STRIDE, 1)

            lax.fori_loop(0, 8, one, expand[...])

    def correlate(pair, nb):
        def one(mb, carry):
            r = pl.ds(pl.multiple_of(mb * 512, 512), 512)
            corr[r, pair * 768 + nb * 256:pair * 768 + (nb + 1) * 256] = jnp.dot(
                filt[r, :], hank[:, nb * 256:(nb + 1) * 256], preferred_element_type=F32).astype(BF)
            return carry

        lax.fori_loop(0, filt.shape[0] // 512, one, 0)

    def pieces(t):
        if t == 0:
            return [(z, 0), (z, 2)], [(z, 1), (z, 3)]
        if t == 7:
            far = (z + 4) % NZ
            return [(far, 0), (far, 2)], [(far, 1), (far, 3)]
        dist, kp = (t + 1) // 2, (t + 1) % 2
        lo, hi = (z + NZ - dist) % NZ, (z + dist) % NZ
        return [(lo, 2 * kp), (hi, 2 * kp)], [(lo, 2 * kp + 1), (hi, 2 * kp + 1)]

    half = 2 * width

    def span_of(p):
        return pl.ds(p * half, half)

    def first(t, p):
        u = t * 2 + p
        cut = (t, slice(None), span_of(p))
        return remote(c1s.at[cut], c1r.at[cut], c1_send.at[u], c1_recv.at[u], at(xl, 1 - core, y, xh, z))

    def second(t, p):
        u = t * 2 + p
        cut = (t, slice(None), span_of(p))
        return remote(c2s.at[cut], c2r.at[cut], c2_send.at[u], c2_recv.at[u], at(1 - xl, core, y, xh, z))

    def project(t, p):
        keep, give = pieces(t)
        left = jnp.concatenate(
            [a_all[zs, k, c] for c in (1 - core, core) for zs, k in keep + give], axis=0)

        cols = span_of(p)
        part = jnp.dot(left, corr[:, cols], preferred_element_type=F32)
        c1s[t, :, cols] = part[:128].astype(BF)
        own[t, :, cols] = part[128:]
        c = first(t, p)
        c.start()
        pending.append(c)

    def halve(t, p):
        first(t, p).wait_recv()
        cols = span_of(p)
        c2s[t, :, cols] = (own[t, 64:128, cols] + c1r[t, 64:128, cols].astype(F32)).astype(BF)
        c = second(t, p)
        c.start()
        pending.append(c)
        own[t, 0:64, cols] = own[t, 0:64, cols] + c1r[t, 0:64, cols].astype(F32)

    def out_rows(t, sub, y_src):
        zs, k = pieces(t)[0][sub]
        return pl.ds(pl.multiple_of(((y_src * 2 + flip(xh, k >> 1)) * NZ + zs) * rows, rows), rows)

    def finish(t, p):
        second(t, p).wait_recv()
        for dy in (2 * p, 2 * p + 1):
            for d in range(3):
                at_ = pl.ds(dy * width + d * LANES, LANES)
                done[t, dy, d] = (own[t, 0:64, at_] + c2r[t, :, at_].astype(F32)).astype(BF)
        for sub in range(2):
            for dy in (2 * p, 2 * p + 1):
                src = done.at[t, dy, :, pl.ds(sub * rows, rows)]
                dst = out_ref.at[:, out_rows(t, sub, y)]
                n = (t * 2 + sub) * NY + dy
                if dy == 0:
                    c = pltpu.make_async_copy(src, dst, keep_sem.at[t * 2 + sub])
                    c.start()
                    kept.append(c)
                else:
                    c = remote(src, dst, c3_send.at[n], c3_recv.at[n], at(xl, core, (y + dy) % NY, xh, z))
                    c.start()
                    pending.append(c)

    kept = []
    hankel(1)
    correlate(1, 0)
    event(1, 2)
    correlate(1, 1)
    correlate(1, 2)
    event(1, 3)
    project(0, 1)
    project(1, 1)
    halve(0, 1)
    project(2, 1)
    halve(1, 1)
    event(2, 0)
    hankel(0)
    halve(2, 1)
    correlate(0, 0)
    event(2, 1)
    project(3, 1)
    correlate(0, 1)
    halve(3, 1)
    finish(0, 1)
    correlate(0, 2)
    project(0, 0)
    project(1, 0)
    halve(0, 0)
    event(2, 2)
    project(2, 0)
    halve(1, 0)
    finish(1, 1)
    project(3, 0)
    halve(2, 0)
    finish(2, 1)
    halve(3, 0)
    event(2, 3)
    project(4, 1)
    project(4, 0)
    halve(4, 1)
    event(3, 0)
    halve(4, 0)
    finish(3, 1)
    finish(0, 0)
    event(3, 1)
    project(5, 1)
    project(5, 0)
    halve(5, 1)
    finish(1, 0)
    finish(2, 0)
    halve(5, 0)
    event(3, 2)
    finish(4, 1)
    finish(3, 0)
    event(3, 3)
    project(6, 1)
    project(6, 0)
    halve(6, 1)
    halve(6, 0)
    finish(4, 0)
    finish(5, 1)
    finish(5, 0)
    event(4, 0)
    event(4, 1)
    event(4, 2)
    event(4, 3)
    project(7, 1)
    project(7, 0)
    halve(7, 1)
    finish(6, 1)
    halve(7, 0)
    finish(6, 0)
    finish(7, 1)
    finish(7, 0)

    for t in range(8):
        for sub in range(2):
            for dy in range(1, NY):
                n = (t * 2 + sub) * NY + dy
                src_y = (y + NY - dy) % NY
                remote(done.at[t, dy, :, pl.ds(sub * rows, rows)], out_ref.at[:, out_rows(t, sub, src_y)],
                       c3_send.at[n], c3_recv.at[n], at(xl, core, y, xh, z)).wait_recv()
    for c in pending:
        c.wait_send()
    for c in kept:
        c.wait()


def shards(strain, basis_filters, coefficients):
    detectors, block_len = strain.shape
    filters_here, taps = basis_filters.shape
    rows, _ = coefficients.shape
    phases = strain.reshape(detectors, block_len // STRIDE, STRIDE).transpose(0, 2, 1)
    phases = jnp.pad(phases.reshape(detectors * STRIDE, block_len // STRIDE), ((0, 16 - detectors * STRIDE), (0, 0)))
    width = detectors * LANES
    cols = NY * width
    out_rows = rows * 64
    dma = pltpu.SemaphoreType.DMA
    out = pl.pallas_call(
        kernel,
        out_shape=jax.ShapeDtypeStruct((detectors, out_rows, LANES), BF),
        in_specs=[
            pl.BlockSpec(memory_space=pltpu.VMEM),
            pl.BlockSpec(memory_space=pl.ANY),
            pl.BlockSpec(memory_space=pl.ANY),
        ],
        out_specs=pl.BlockSpec(memory_space=pltpu.VMEM),
        scratch_shapes=[
            pltpu.VMEM((NZ, 4, 2, rows, filters_here), BF),
            pltpu.VMEM((NY + 1, 2, 16, LANES), BF),
            pltpu.VMEM((4, NY, 16, LANES), BF),
            pltpu.VMEM((filters_here, taps), BF),
            pltpu.VMEM((taps, 2 * width), BF),
            pltpu.VMEM((48, 5 * LANES), F32),
            pltpu.VMEM((filters_here, cols), BF),
            pltpu.VMEM((8, 128, cols), BF),
            pltpu.VMEM((8, 128, cols), BF),
            pltpu.VMEM((8, 128, cols), F32),
            pltpu.VMEM((8, 64, cols), BF),
            pltpu.VMEM((8, 64, cols), BF),
            pltpu.VMEM((8, NY, detectors, 64, LANES), BF),
            dma((4,)),
            dma((8,)), dma((8,)), dma((8,)), dma((8,)), dma((8,)), dma((8,)),
            dma((2, 4, 4)), dma((2, 4, 4)),
            dma((16,)), dma((16,)), dma((16,)), dma((16,)),
            dma((64,)), dma((64,)), dma((16,)),
        ],
        compiler_params=pltpu.CompilerParams(
            collective_id=0, has_side_effects=True, vmem_limit_bytes=60 * 1024 * 1024),
    )(phases, basis_filters, coefficients)
    return out.transpose(1, 0, 2)


def solution(mesh):
    placed = (P(None, "tm"), P("basis", None), P(("basis", "tm"), None))
    return jax.shard_map(
        shards, mesh=mesh, in_specs=placed, out_specs=P("basis", None, "tm"), check_vma=False
    )
```
